32 devices in a mesh: leaf: 8 (over z, core), probe: 4 (over y, x).
Axes of the slice: x: 2, y: 2, z: 4, core: 2. Of those that a mesh axis runs over, the one named last changes fastest.
Arguments:
- points: bfloat16 [8, 32768], P(None, 'leaf'), may hold values from -6 to 6
- values: bfloat16 [64, 32768], P('probe', 'leaf'), may hold values from -6 to 6
- order: int32 [8, 4096], P('leaf'), may hold values from 0 to 4095, each once within a row
- block_list: int32 [128, 8], P('leaf'), may hold values from 0 to 127, as said below
- leaf_basis: bfloat16 [128, 256, 256], P('leaf'), may hold values from -0.375 to 0.375
- local_transfers: bfloat16 [8, 30, 2, 256, 256], P('leaf'), may hold values from -0.25 to 0.25
- chain_transfers: bfloat16 [8, 3, 2, 256, 256], P('leaf', None, None, 'probe'), as said below
Outputs:
- product: float32 [64, 32768], P('probe', 'leaf')
The draws below stay inside these ranges and needn't reach their ends.
Inputs may be any that keep to these rules, and one draw needn't show every extreme that they name: `block_list`: row i lists leaf i first, then 8 - 1 leaves j with 1 <= |j - i| <= 16; entries may repeat. `order`: each row is a permutation. `chain_transfers`: slot j of device d holds the pair of the level 4 + j node above d; all devices under one node hold the same pair.
All inputs are finite; a program needn't handle non-finite values.
Results may differ from the reference program's by a relative error of at most 0.0028.
Values may be sent and summed in bfloat16 or wider, within the bound.
A program may use at most 64 MiB of HBM per device.

```python
import jax
import jax.numpy as jnp
import numpy as np
from jax import lax

DIM = 8
LEAF = 256
RANK = 256
PROBES = 64
NEAR = 8
LOCAL = 4
LEAF_DEV = 16
CHAIN = 3
LEAVES = 128
PTS_DEV = 4096
POINTS = 32768
LOCAL_NODES = 30
N_LEAF = 8


def draw_block_list(key, part):
    nonzero = jnp.concatenate([-jnp.arange(1, LEAF_DEV + 1, dtype=jnp.int32), jnp.arange(1, LEAF_DEV + 1, dtype=jnp.int32)])
    row_keys = jax.random.split(key, LEAVES)
    offsets = jax.vmap(lambda subkey: jax.random.permutation(subkey, nonzero)[:NEAR - 1])(row_keys)
    offsets = offsets.at[0, 0].set(LEAF_DEV)
    itself = jnp.arange(LEAVES, dtype=jnp.int32)[:, None]
    forward = itself + offsets
    inside = jnp.logical_and(forward >= 0, forward < LEAVES)
    picked = jnp.where(inside, forward, itself - offsets)
    return jnp.concatenate([itself, picked], 1).astype(jnp.int32)


def draw_chain_transfers(key, part):
    devices = np.arange(N_LEAF)
    owners = np.stack([devices >> level_shift << level_shift for level_shift in range(CHAIN)], 1)
    node_table = owners * CHAIN + np.arange(CHAIN)[None, :]

    def one_device(node_ids):

        def one_node(node_index):
            node_key = jax.random.fold_in(key, node_index)
            sample = jax.random.normal(node_key, (2, RANK, RANK), jnp.float32)
            return (sample * (2.0 * RANK) ** (-0.5)).astype(jnp.bfloat16)
        return jax.vmap(one_node)(node_ids)
    return lax.map(one_device, jnp.asarray(node_table, dtype=jnp.int32))


def level_of(rng, dims, pieces, least, largest):
    def one(dim, shards_of):
        draws = jax.random.uniform(jax.random.fold_in(jax.random.fold_in(rng, 6), dim), (shards_of,), jnp.float32, least / len(pieces), largest / len(pieces))
        return jnp.repeat(jnp.exp(draws), dims[dim] // shards_of).reshape((-1,) + (1,) * (len(dims) - dim - 1))

    factor_of = one(*pieces[0])
    for cut in pieces[1:]:
        factor_of = factor_of * one(*cut)
    return factor_of


def normal_values(stream_key, dims, width, bound, cuts=(), kind=jnp.bfloat16):
    loudness = level_of(stream_key, dims, cuts, -0.22, 0.18) if cuts else 1.0
    entries = jax.random.normal(stream_key, dims, jnp.float32) * width * loudness
    return jnp.minimum(jnp.maximum(entries, -bound), bound).astype(kind)


def setup_inputs(seed: int = 0) -> dict:
    key_list = jax.random.split(jax.random.key(seed), 8)
    return {
        "points": normal_values(key_list[0], (DIM, POINTS), 1.0, 6.0, ((1, 8),)),
        "values": normal_values(key_list[1], (PROBES, POINTS), 1.0, 6.0, ((0, 4), (1, 8))),
        "order": jax.vmap(lambda own: jax.random.permutation(own, PTS_DEV))(jax.random.split(key_list[2], N_LEAF)).reshape((N_LEAF, PTS_DEV)).astype(jnp.int32),
        "block_list": draw_block_list(jax.random.fold_in(key_list[7], 71), 0),
        "leaf_basis": normal_values(key_list[4], (LEAVES, LEAF, RANK), LEAF ** -0.5, 0.375, ((0, 8),)),
        "local_transfers": normal_values(key_list[5], (N_LEAF, LOCAL_NODES, 2, RANK, RANK), (2 * RANK) ** -0.5, 0.25, ((0, 8),)),
        "chain_transfers": draw_chain_transfers(jax.random.fold_in(key_list[7], 71), 0),
    }


PRECISE = lax.Precision.HIGHEST


def kernel_tile(source, target):
    source = source.astype(jnp.float32)
    target = target.astype(jnp.float32)
    inner_prod = jnp.einsum("dnq,dp->nqp", source, target, precision=PRECISE)
    squared = jnp.sum(source * source, 0)[:, :, None] + jnp.sum(target * target, 0)[None, None, :] - 2.0 * inner_prod
    factor = 1.0 + squared * 0.125
    return 1.0 / (factor * factor * factor)


def pair_fields(partial_value):
    upward = partial_value[:, 0]
    coupled = partial_value[:, 1]
    node_count = upward.shape[0]
    merged = upward[0::2] + upward[1::2]
    crossed = coupled.reshape(node_count // 2, 2, coupled.shape[1], coupled.shape[2])[:, ::-1].reshape(coupled.shape)
    return merged, crossed


def lift_terms(matrices, skeleton):
    return jnp.einsum("nmab,nac->nmbc", matrices.astype(jnp.float32), skeleton, precision=PRECISE)


def push_down(matrices, parent):
    return jnp.einsum("nab,nbc->nac", matrices.astype(jnp.float32), parent, precision=PRECISE)


def reference(points, values, order, block_list, leaf_basis, local_transfers, chain_transfers):
    positions = (order + (jnp.arange(N_LEAF, dtype=jnp.int32) * PTS_DEV)[:, None]).reshape(-1).astype(jnp.int32)
    coords = jnp.take(points, positions, axis=1).reshape(DIM, LEAVES, LEAF)
    values_tree = jnp.take(values, positions, axis=1).reshape(PROBES, LEAVES, LEAF)

    def near_leaf(leaf_index):
        picked_coords = jnp.take(coords, block_list[leaf_index], axis=1)
        picked_values = jnp.take(values_tree, block_list[leaf_index], axis=1)
        own_coords = lax.dynamic_index_in_dim(coords, leaf_index, 1, keepdims=False)
        near_tile = kernel_tile(picked_coords, own_coords).astype(jnp.bfloat16)
        return jnp.einsum("cnq,nqp->cp", picked_values.astype(jnp.float32), near_tile.astype(jnp.float32), precision=PRECISE)

    near_part = lax.map(near_leaf, jnp.arange(LEAVES, dtype=jnp.int32))
    skeleton = jnp.einsum("lqr,clq->lrc", leaf_basis.astype(jnp.float32), values_tree.astype(jnp.float32), precision=PRECISE)
    fields = []
    slot_start = 0
    for tree_level in range(LOCAL):
        node_count = LEAF_DEV >> tree_level
        matrices = local_transfers[:, slot_start:slot_start + node_count].reshape(N_LEAF * node_count, 2, RANK, RANK)
        skeleton, crossed = pair_fields(lift_terms(matrices, skeleton))
        fields.append(crossed)
        slot_start += node_count
    for chain_step in range(CHAIN):
        matrices = chain_transfers[::2 ** chain_step, chain_step]
        skeleton, crossed = pair_fields(lift_terms(matrices, skeleton))
        fields.append(crossed)
    node_field = jnp.zeros((1, RANK, PROBES), jnp.float32)
    for chain_step in range(CHAIN - 1, -1, -1):
        matrices = chain_transfers[::2 ** chain_step, chain_step, 0]
        node_field = fields[LOCAL + chain_step] + push_down(matrices, jnp.repeat(node_field, 2, axis=0))
    slot_start = 2 * LEAF_DEV - 2
    for tree_level in range(LOCAL - 1, -1, -1):
        node_count = LEAF_DEV >> tree_level
        slot_start -= node_count
        matrices = local_transfers[:, slot_start:slot_start + node_count, 0].reshape(N_LEAF * node_count, RANK, RANK)
        node_field = fields[tree_level] + push_down(matrices, jnp.repeat(node_field, 2, axis=0))
    far_part = jnp.einsum("lqr,lrc->clq", leaf_basis.astype(jnp.float32), node_field, precision=PRECISE)
    combined = jnp.transpose(near_part, (1, 0, 2)) + far_part
    flattened = combined.reshape(PROBES, POINTS)
    return jnp.zeros_like(flattened).at[:, positions].set(flattened)
```

```python
import functools

import jax
import jax.numpy as jnp
from jax import lax
from jax.experimental import pallas as pl
from jax.experimental.pallas import tpu as pltpu
from jax.sharding import PartitionSpec as P

F32 = jnp.float32
BF16 = jnp.bfloat16
NN = (((1,), (0,)), ((), ()))
NT = (((1,), (1,)), ((), ()))
GW = 4
NW = 2
SW = 8
KW = 8
PW = 4
EARLY = 2


def split2(x):
    hi = x.astype(BF16)
    lo = (x - hi.astype(F32)).astype(BF16)
    return jnp.concatenate([hi, lo], axis=0)


def dot(a, b, dims=NN):
    return lax.dot_general(a, b, dims, preferred_element_type=F32)


def dot2(x2, b, dims=NN):
    rows = x2.shape[0] // 2
    out = dot(x2, b, dims)
    return out[:rows] + out[rows:]


def several(first, last, width, step):
    count = (last - first) // width

    def trip(i, carry):
        for u in range(width):
            step(first + i * width + u)
        return carry

    lax.fori_loop(0, count, trip, 0)
    for left in range(first + count * width, last):
        step(left)


def tree_kernel(
    leaf_count, probe_count, chain_depth, near_count,
    blocks_hbm, points_hbm, values_hbm, order_hbm, basis_hbm, local_hbm, chain_hbm,
    out_ref,
    blocks, points, values, order, stacked, coords, window, target, basis, local, chain,
    skel, field, near, chain_out, chain_in,
    first_sem, local_sem, probe_send, probe_recv, share_send, share_recv, pass_send, pass_recv,
    halo_send, halo_recv, chain_send, chain_recv,
):
    leaf_dev, leaf_size, rank = basis.shape
    dim = points.shape[0]
    cols = values.shape[0]
    rows = chain_hbm.shape[2]
    levels = leaf_dev.bit_length() - 1
    me = lax.axis_index("leaf")
    mine = lax.axis_index("probe")

    barrier = pltpu.get_barrier_semaphore()
    for k in range(1, leaf_count):
        pl.semaphore_signal(
            barrier, inc=1,
            device_id=(lax.rem(me + k, leaf_count), mine), device_id_type=pl.DeviceIdType.MESH,
        )
    for k in range(1, probe_count):
        pl.semaphore_signal(
            barrier, inc=1,
            device_id=(me, lax.rem(mine + k, probe_count)), device_id_type=pl.DeviceIdType.MESH,
        )

    arrays = ((values_hbm, values), (points_hbm, points), (order_hbm, order), (blocks_hbm, blocks))
    inputs = [
        pltpu.make_async_copy(src, dst, first_sem.at[i]) for i, (src, dst) in enumerate(arrays)
    ]
    for load in inputs:
        load.start()
    loads = [pltpu.make_async_copy(basis_hbm, basis, local_sem.at[0])]
    start = 0
    for level in range(levels):
        count = leaf_dev >> level
        part = pl.ds(start, count)
        loads.append(
            pltpu.make_async_copy(local_hbm.at[part], local.at[part], local_sem.at[1 + level])
        )
        start += count
    chain_part = chain.at[:, :, pl.ds(pl.multiple_of(mine * rows, rows), rows), :]
    loads.append(pltpu.make_async_copy(chain_hbm, chain_part, local_sem.at[1 + levels]))
    for load in loads:
        load.start()

    pl.semaphore_wait(barrier, leaf_count - 1 + probe_count - 1)
    core = lax.rem(me, 2)
    twin = me + 1 - 2 * core
    kind = 1 - core
    last = chain_depth - 1

    def remote(src, dst, send, recv, leaf, probe):
        return pltpu.make_async_remote_copy(
            src_ref=src, dst_ref=dst, send_sem=send, recv_sem=recv,
            device_id=(leaf, probe), device_id_type=pl.DeviceIdType.MESH,
        )

    def rows_of(owner):
        return pl.ds(pl.multiple_of(owner * rows, rows), rows)

    gathers, shared, passed = [], [], []
    for k in range(1, probe_count):
        peer = lax.rem(mine + k, probe_count)
        source = lax.rem(mine + probe_count - k, probe_count)
        for step in range(1, chain_depth):
            slot = (k - 1) * last + step - 1
            shared.append(
                remote(
                    chain_hbm.at[step, kind], chain.at[step, kind, rows_of(mine)],
                    share_send.at[slot], share_recv.at[slot], me, peer,
                )
            )
            arrived = chain.at[step, kind, rows_of(source)]
            passed.append(
                remote(arrived, arrived, pass_send.at[slot], pass_recv.at[slot], twin, mine)
            )
        gathers.append(
            remote(
                chain_hbm.at[0], chain.at[0, :, rows_of(mine)],
                probe_send.at[k - 1], probe_recv.at[k - 1], me, peer,
            )
        )

    def top(i):
        return i % last == last - 1

    def each_sent(copies, act):
        for i, copy in enumerate(copies):
            if not top(i):
                act(copy)

        @pl.when(core == 0)
        def _():
            for i, copy in enumerate(copies):
                if top(i):
                    act(copy)

    def each_passed_in(act):
        for i, copy in enumerate(passed):
            if not top(i):
                act(copy)

        @pl.when(core == 1)
        def _():
            for i, copy in enumerate(passed):
                if top(i):
                    act(copy)

    each_sent(shared, lambda copy: copy.start())
    for copy in gathers:
        copy.start()

    for load in inputs:
        load.wait()
    for h in range(leaf_dev):
        piece = slice(h * leaf_size, (h + 1) * leaf_size)
        stacked[h * cols : (h + 1) * cols, :] = values[:, piece]
    stacked[leaf_dev * cols :, :] = jnp.concatenate(
        [
            points[:, h * leaf_size : (h + 1) * leaf_size].astype(F32)
            for h in range(leaf_dev)
        ],
        axis=0,
    ).astype(BF16)

    wide = GW * leaf_size
    row_id = lax.broadcasted_iota(jnp.int32, (leaf_size, wide), 0)
    tail_row = lax.broadcasted_iota(jnp.int32, (8, leaf_size), 0)

    def augment(l):
        x = coords[l]
        norm = jnp.sum(x * x, axis=0, keepdims=True) * 0.125
        n1 = norm.astype(BF16).astype(F32)
        n2 = (norm - n1).astype(BF16).astype(F32)
        n3 = norm - n1 - n2
        one = jnp.where(tail_row < 7, 1.0, 0.0)
        src_tail = jnp.where(
            tail_row == 0, n1, jnp.where(tail_row == 1, n2, jnp.where(tail_row == 2, n3, one))
        )
        own_tail = jnp.where(
            tail_row == 3, n1, jnp.where(tail_row == 4, n2, jnp.where(tail_row == 5, n3, one))
        )
        window[leaf_dev + l, :16, :] = jnp.concatenate([x, src_tail], axis=0).astype(BF16)
        target[l] = jnp.concatenate([x * -0.25, own_tail], axis=0).T.astype(BF16)

    def gather_leaves(i):
        piece = slice(i * wide, (i + 1) * wide)
        where_to = order[:, piece]
        low = where_to % leaf_size
        high = where_to // leaf_size
        hot = jnp.where(row_id == low, 1.0, 0.0).astype(BF16)
        found = dot(stacked[...], hot)
        vals = jnp.zeros((cols, wide), F32)
        x = jnp.zeros((dim, wide), F32)
        for h in range(leaf_dev):
            here = high == h
            vals = jnp.where(here, found[h * cols : (h + 1) * cols], vals)
            base = leaf_dev * cols + h * dim
            x = jnp.where(here, found[base : base + dim], x)
        for u in range(GW):
            part = slice(u * leaf_size, (u + 1) * leaf_size)
            coords[i * GW + u] = x[:, part]
            window[leaf_dev + i * GW + u, 16:, :] = vals[:, part].astype(BF16)
            augment(i * GW + u)

    to_right, to_left = [], []
    for i in range(leaf_dev // GW):
        gather_leaves(i)
        own = window.at[pl.ds(leaf_dev + i * GW, GW)]
        to_right.append(
            remote(
                own, window.at[pl.ds(i * GW, GW)], halo_send.at[0, i], halo_recv.at[0, i],
                lax.rem(me + 1, leaf_count), mine,
            )
        )
        to_left.append(
            remote(
                own, window.at[pl.ds(2 * leaf_dev + i * GW, GW)], halo_send.at[1, i],
                halo_recv.at[1, i], lax.rem(me + leaf_count - 1, leaf_count), mine,
            )
        )
        pl.when(me < leaf_count - 1)(to_right[i].start)
        pl.when(me > 0)(to_left[i].start)

    def lift_pair(j):
        first, second = split2(skel[2 * j]), split2(skel[2 * j + 1])
        skel[leaf_dev + j] = dot2(first, local[2 * j, 0]) + dot2(second, local[2 * j + 1, 0])
        field[2 * j + 1] = dot2(first, local[2 * j, 1])
        field[2 * j] = dot2(second, local[2 * j + 1, 1])

    def over_pairs(first, count, step):
        width = min(count, 4)

        def trip(i, carry):
            for u in range(width):
                step(first + i * width + u)
            return carry

        if count == width:
            trip(0, 0)
        else:
            lax.fori_loop(0, count // width, trip, 0)

    def leaf_skeleton(l):
        skel[l] = dot(window[leaf_dev + l, 16:, :], basis[l])

    loads[0].wait()
    several(0, leaf_dev, KW, leaf_skeleton)

    first = 0
    for level in range(levels):
        loads[1 + level].wait()
        count = leaf_dev >> (level + 1)
        over_pairs(first, count, lift_pair)
        first += count

    def spread_chain():
        now2 = split2(skel[2 * leaf_dev - 2])
        copies = []
        for step in range(chain_depth):
            chain_out[step] = dot2(now2, chain[step, 1]).astype(BF16)
            count = 2**step
            place = lax.rem(me, count)
            across = me // count
            across = (across + 1 - 2 * lax.rem(across, 2)) * count
            for k in range(count):
                copies.append(
                    remote(
                        chain_out.at[step], chain_in.at[count - 1 + place],
                        chain_send.at[count - 1 + k], chain_recv.at[count - 1 + place],
                        across + lax.rem(place + k, count), mine,
                    )
                )
                copies[-1].start()
            if step < last:
                now2 = split2(dot2(now2, chain[step, 0]))
        return copies

    loads[1 + levels].wait()
    each_sent(shared, lambda copy: copy.wait_recv())
    each_sent(passed, lambda copy: copy.start())

    @pl.when(me > 0)
    def _():
        for copy in to_right:
            copy.wait_recv()

    @pl.when(me < leaf_count - 1)
    def _():
        for copy in to_left:
            copy.wait_recv()

    base_leaf = me * leaf_dev - leaf_dev

    def near_group(i, carry):
        group = [i * NW + u for u in range(NW)]
        own_sides = [target[l] for l in group]
        totals = [jnp.zeros((cols, leaf_size), F32) for _ in group]
        waiting = None
        for n in range(near_count + 1):
            made = []
            if n < near_count:
                for l, own_side in zip(group, own_sides):
                    slot = jnp.clip(blocks[n, l] - base_leaf, 0, 3 * leaf_dev - 1)
                    factor = dot(own_side, window[slot, :16, :])
                    made.append((slot, (1.0 / (factor * factor * factor)).astype(BF16)))
            if waiting:
                for u, (slot, tile) in enumerate(waiting):
                    totals[u] += dot(window[slot, 16:, :], tile, NT)
            waiting = made
        for l, total in zip(group, totals):
            near[l] = total
        return carry

    trips = leaf_dev // NW
    early = trips * EARLY // 8
    lax.fori_loop(0, early, near_group, 0)
    for copy in gathers:
        copy.wait_recv()
    each_passed_in(lambda copy: copy.wait_recv())
    exchange = spread_chain()
    lax.fori_loop(early, trips, near_group, 0)
    for slot in range(leaf_count - 1):
        remote(
            chain_out.at[0], chain_in.at[slot], chain_send.at[slot], chain_recv.at[slot], twin, mine
        ).wait_recv()

    def coupling(step):
        first_slot = 2**step - 1
        total = chain_in[first_slot].astype(F32)
        for slot in range(first_slot + 1, 2 * first_slot + 1):
            total = total + chain_in[slot].astype(F32)
        return total

    node = coupling(last)
    for step in range(last - 1, -1, -1):
        node = coupling(step) + dot2(split2(node), chain[step, 0], NT)
    field[2 * leaf_dev - 2] = node

    def push_pair(j):
        parent = split2(field[leaf_dev + j])
        for child in (2 * j, 2 * j + 1):
            field[child] = field[child] + dot2(parent, local[child, 0], NT)

    for level in range(levels - 1, -1, -1):
        count = leaf_dev >> (level + 1)
        first -= count
        over_pairs(first, count, push_pair)

    def finish_leaf(l):
        out_ref[l] = (near[l] + dot2(split2(field[l]), basis[l], NT)).astype(BF16)

    several(0, leaf_dev, SW, finish_leaf)

    for copy in gathers + exchange:
        copy.wait_send()
    each_sent(shared, lambda copy: copy.wait_send())
    each_sent(passed, lambda copy: copy.wait_send())

    @pl.when(me < leaf_count - 1)
    def _():
        for copy in to_right:
            copy.wait_send()

    @pl.when(me > 0)
    def _():
        for copy in to_left:
            copy.wait_send()


def place_kernel(order_hbm, tree_hbm, out_ref, placed, order, tree, sems):
    loads = [
        pltpu.make_async_copy(order_hbm, order, sems.at[0]),
        pltpu.make_async_copy(tree_hbm, tree, sems.at[1]),
    ]
    for load in loads:
        load.start()
    loads[0].wait()
    leaf_dev, cols, leaf_size = tree.shape
    wide = PW * leaf_size
    row_id = lax.broadcasted_iota(jnp.int32, (leaf_size, wide), 0)
    for i in range(leaf_dev // PW):
        where_to = order[:, i * wide : (i + 1) * wide]
        hot = jnp.where(row_id == where_to % leaf_size, 1.0, 0.0).astype(BF16)
        high = where_to // leaf_size
        if i == 0:
            loads[1].wait()
        mine = jnp.concatenate([tree[i * PW + u].astype(F32) for u in range(PW)], axis=1)
        spread = jnp.concatenate(
            [jnp.where(high == h, mine, 0.0).astype(BF16) for h in range(leaf_dev)], axis=0
        )
        term = dot(spread, hot, NT)
        if i == 0:
            placed[...] = term
        elif i < leaf_dev // PW - 1:
            placed[...] += term
        else:
            for h in range(leaf_dev):
                rows = slice(h * cols, (h + 1) * cols)
                out_ref[:, h * leaf_size : (h + 1) * leaf_size] = placed[rows] + term[rows]


def shards(points, values, order, block_list, leaf_basis, local_transfers, chain_transfers):
    leaf_dev, leaf_size, rank = leaf_basis.shape
    leaf_count = lax.axis_size("leaf")
    probe_count = lax.axis_size("probe")
    depth = leaf_count.bit_length() - 1
    columns = values.shape[0]
    cols = -(-columns // 16) * 16
    if cols != columns:
        values = jnp.pad(values, ((0, cols - columns), (0, 0)))
    dim = points.shape[0]
    levels = leaf_dev.bit_length() - 1
    nodes = 2 * leaf_dev
    vmem = pl.BlockSpec(memory_space=pltpu.VMEM)
    anywhere = pl.BlockSpec(memory_space=pl.ANY)
    tree = pl.pallas_call(
        functools.partial(tree_kernel, leaf_count, probe_count, depth, block_list.shape[1]),
        out_shape=jax.ShapeDtypeStruct((leaf_dev, cols, leaf_size), BF16),
        in_specs=[anywhere] * 7,
        out_specs=vmem,
        scratch_shapes=[
            pltpu.SMEM(block_list.shape[::-1], jnp.int32),
            pltpu.VMEM(points.shape, BF16),
            pltpu.VMEM(values.shape, BF16),
            pltpu.VMEM(order.shape, jnp.int32),
            pltpu.VMEM((leaf_dev * (cols + dim), leaf_size), BF16),
            pltpu.VMEM((leaf_dev, dim, leaf_size), F32),
            pltpu.VMEM((3 * leaf_dev, 16 + cols, leaf_size), BF16),
            pltpu.VMEM((leaf_dev, leaf_size, 16), BF16),
            pltpu.VMEM(leaf_basis.shape, BF16),
            pltpu.VMEM(local_transfers.shape[1:], BF16),
            pltpu.VMEM((depth, 2, rank, rank), BF16),
            pltpu.VMEM((nodes, cols, rank), F32),
            pltpu.VMEM((nodes, cols, rank), F32),
            pltpu.VMEM((leaf_dev, cols, leaf_size), F32),
            pltpu.VMEM((depth, cols, rank), BF16),
            pltpu.VMEM((leaf_count - 1, cols, rank), BF16),
            pltpu.SemaphoreType.DMA((4,)),
            pltpu.SemaphoreType.DMA((levels + 2,)),
            pltpu.SemaphoreType.DMA((probe_count - 1,)),
            pltpu.SemaphoreType.DMA((probe_count - 1,)),
            pltpu.SemaphoreType.DMA(((probe_count - 1) * (depth - 1),)),
            pltpu.SemaphoreType.DMA(((probe_count - 1) * (depth - 1),)),
            pltpu.SemaphoreType.DMA(((probe_count - 1) * (depth - 1),)),
            pltpu.SemaphoreType.DMA(((probe_count - 1) * (depth - 1),)),
            pltpu.SemaphoreType.DMA((2, leaf_dev // GW)),
            pltpu.SemaphoreType.DMA((2, leaf_dev // GW)),
            pltpu.SemaphoreType.DMA((leaf_count - 1,)),
            pltpu.SemaphoreType.DMA((leaf_count - 1,)),
        ],
        compiler_params=pltpu.CompilerParams(
            collective_id=0, has_side_effects=True, vmem_limit_bytes=60 * 1024 * 1024
        ),
        name="tree_product",
    )(block_list.T, points, values, order, leaf_basis, local_transfers[0], chain_transfers[0])
    product = pl.pallas_call(
        place_kernel,
        out_shape=jax.ShapeDtypeStruct((cols, leaf_dev * leaf_size), F32),
        in_specs=[anywhere] * 2,
        out_specs=vmem,
        scratch_shapes=[
            pltpu.VMEM((leaf_dev * cols, leaf_size), F32),
            pltpu.VMEM(order.shape, jnp.int32),
            pltpu.VMEM(tree.shape, BF16),
            pltpu.SemaphoreType.DMA((2,)),
        ],
        compiler_params=pltpu.CompilerParams(vmem_limit_bytes=60 * 1024 * 1024),
        name="place",
    )(order, tree)
    return product[:columns]


def solution(mesh):
    placed = (
        P(None, "leaf"),
        P("probe", "leaf"),
        P("leaf", None),
        P("leaf", None),
        P("leaf", None, None),
        P("leaf", None, None, None, None),
        P("leaf", None, None, "probe", None),
    )
    return jax.shard_map(
        shards, mesh=mesh, in_specs=placed, out_specs=P("probe", "leaf"), check_vma=False
    )
```

```python
import functools

import jax
import jax.numpy as jnp
from jax import lax
from jax.experimental import pallas as pl
from jax.experimental.pallas import tpu as pltpu
from jax.sharding import PartitionSpec as P

F32 = jnp.float32
BF16 = jnp.bfloat16
NN = (((1,), (0,)), ((), ()))
NT = (((1,), (1,)), ((), ()))
GW = 4
NW = 4
SW = 16
KW = 16
PW = 4
ENTER = 0
FIRST = 0
SECOND = 1


def split2(x):
    hi = x.astype(BF16)
    lo = (x - hi.astype(F32)).astype(BF16)
    return jnp.concatenate([hi, lo], axis=0)


def dot(a, b, dims=NN):
    return lax.dot_general(a, b, dims, preferred_element_type=F32)


def dot2(x2, b, dims=NN):
    rows = x2.shape[0] // 2
    out = dot(x2, b, dims)
    return out[:rows] + out[rows:]


def several(first, last, width, step):
    count = (last - first) // width

    def trip(i, carry):
        for u in range(width):
            step(first + i * width + u)
        return carry

    lax.fori_loop(0, count, trip, 0)
    for left in range(first + count * width, last):
        step(left)


def tree_kernel(
    leaf_count, probe_count, chain_depth, near_count,
    blocks_hbm, points_hbm, values_hbm, order_hbm, basis_hbm, local_hbm, chain_hbm,
    out_ref,
    blocks, points, values, order, stacked, coords, window, target, basis, local, chain,
    skel, field, near, chain_out, chain_in,
    first_sem, local_sem, probe_send, probe_recv, share_send, share_recv, pass_send, pass_recv,
    halo_send, halo_recv, chain_send, chain_recv,
):
    leaf_dev, leaf_size, rank = basis.shape
    dim = points.shape[0]
    cols = values.shape[0]
    rows = chain_hbm.shape[2]
    levels = leaf_dev.bit_length() - 1
    me = lax.axis_index("leaf")
    mine = lax.axis_index("probe")

    barrier = pltpu.get_barrier_semaphore()
    for k in range(1, leaf_count):
        pl.semaphore_signal(
            barrier, inc=1,
            device_id=(lax.rem(me + k, leaf_count), mine), device_id_type=pl.DeviceIdType.MESH,
        )
    for k in range(1, probe_count):
        pl.semaphore_signal(
            barrier, inc=1,
            device_id=(me, lax.rem(mine + k, probe_count)), device_id_type=pl.DeviceIdType.MESH,
        )

    arrays = ((values_hbm, values), (points_hbm, points), (order_hbm, order), (blocks_hbm, blocks))
    inputs = [
        pltpu.make_async_copy(src, dst, first_sem.at[i]) for i, (src, dst) in enumerate(arrays)
    ]
    for load in inputs:
        load.start()
    loads = [pltpu.make_async_copy(basis_hbm, basis, local_sem.at[0])]
    start = 0
    for level in range(levels):
        count = leaf_dev >> level
        part = pl.ds(start, count)
        loads.append(
            pltpu.make_async_copy(local_hbm.at[part], local.at[part], local_sem.at[1 + level])
        )
        start += count
    chain_part = chain.at[:, :, pl.ds(pl.multiple_of(mine * rows, rows), rows), :]
    loads.append(pltpu.make_async_copy(chain_hbm, chain_part, local_sem.at[1 + levels]))
    for load in loads:
        load.start()

    core = lax.rem(me, 2)
    twin = me + 1 - 2 * core
    kind = 1 - core
    last = chain_depth - 1

    def remote(src, dst, send, recv, leaf, probe):
        return pltpu.make_async_remote_copy(
            src_ref=src, dst_ref=dst, send_sem=send, recv_sem=recv,
            device_id=(leaf, probe), device_id_type=pl.DeviceIdType.MESH,
        )

    def rows_of(owner):
        return pl.ds(pl.multiple_of(owner * rows, rows), rows)

    gathers, shared, passed = [], [], []
    for k in range(1, probe_count):
        peer = lax.rem(mine + k, probe_count)
        source = lax.rem(mine + probe_count - k, probe_count)
        for step in range(1, chain_depth):
            slot = (k - 1) * last + step - 1
            shared.append(
                remote(
                    chain_hbm.at[step, kind], chain.at[step, kind, rows_of(mine)],
                    share_send.at[slot], share_recv.at[slot], me, peer,
                )
            )
            arrived = chain.at[step, kind, rows_of(source)]
            passed.append(
                remote(arrived, arrived, pass_send.at[slot], pass_recv.at[slot], twin, mine)
            )
        gathers.append(
            remote(
                chain_hbm.at[0], chain.at[0, :, rows_of(mine)],
                probe_send.at[k - 1], probe_recv.at[k - 1], me, peer,
            )
        )

    def top(i):
        return i % last == last - 1

    def each_sent(copies, act):
        for i, copy in enumerate(copies):
            if not top(i):
                act(copy)

        @pl.when(core == 0)
        def _():
            for i, copy in enumerate(copies):
                if top(i):
                    act(copy)

    def each_passed_in(act):
        for i, copy in enumerate(passed):
            if not top(i):
                act(copy)

        @pl.when(core == 1)
        def _():
            for i, copy in enumerate(passed):
                if top(i):
                    act(copy)


    for load in inputs:
        load.wait()
    for h in range(leaf_dev):
        piece = slice(h * leaf_size, (h + 1) * leaf_size)
        stacked[h * cols : (h + 1) * cols, :] = values[:, piece]
    stacked[leaf_dev * cols :, :] = jnp.concatenate(
        [
            points[:, h * leaf_size : (h + 1) * leaf_size].astype(F32)
            for h in range(leaf_dev)
        ],
        axis=0,
    ).astype(BF16)

    wide = GW * leaf_size
    row_id = lax.broadcasted_iota(jnp.int32, (leaf_size, wide), 0)
    tail_row = lax.broadcasted_iota(jnp.int32, (8, leaf_size), 0)

    def augment(l):
        x = coords[l]
        norm = jnp.sum(x * x, axis=0, keepdims=True) * 0.125
        n1 = norm.astype(BF16).astype(F32)
        n2 = (norm - n1).astype(BF16).astype(F32)
        n3 = norm - n1 - n2
        one = jnp.where(tail_row < 7, 1.0, 0.0)
        src_tail = jnp.where(
            tail_row == 0, n1, jnp.where(tail_row == 1, n2, jnp.where(tail_row == 2, n3, one))
        )
        own_tail = jnp.where(
            tail_row == 3, n1, jnp.where(tail_row == 4, n2, jnp.where(tail_row == 5, n3, one))
        )
        window[leaf_dev + l, :16, :] = jnp.concatenate([x, src_tail], axis=0).astype(BF16)
        target[l] = jnp.concatenate([x * -0.25, own_tail], axis=0).T.astype(BF16)

    def gather_leaves(i):
        piece = slice(i * wide, (i + 1) * wide)
        where_to = order[:, piece]
        low = where_to % leaf_size
        high = where_to // leaf_size
        hot = jnp.where(row_id == low, 1.0, 0.0).astype(BF16)
        found = dot(stacked[...], hot)
        vals = jnp.zeros((cols, wide), F32)
        x = jnp.zeros((dim, wide), F32)
        for h in range(leaf_dev):
            here = high == h
            vals = jnp.where(here, found[h * cols : (h + 1) * cols], vals)
            base = leaf_dev * cols + h * dim
            x = jnp.where(here, found[base : base + dim], x)
        for u in range(GW):
            part = slice(u * leaf_size, (u + 1) * leaf_size)
            coords[i * GW + u] = x[:, part]
            window[leaf_dev + i * GW + u, 16:, :] = vals[:, part].astype(BF16)
            augment(i * GW + u)

    def enter():
        pl.semaphore_wait(barrier, leaf_count - 1 + probe_count - 1)
        each_sent(shared, lambda copy: copy.start())
        for copy in gathers:
            copy.start()

    def send_leaves(i):
        own = window.at[pl.ds(leaf_dev + i * GW, GW)]
        to_right.append(
            remote(
                own, window.at[pl.ds(i * GW, GW)], halo_send.at[0, i], halo_recv.at[0, i],
                lax.rem(me + 1, leaf_count), mine,
            )
        )
        to_left.append(
            remote(
                own, window.at[pl.ds(2 * leaf_dev + i * GW, GW)], halo_send.at[1, i],
                halo_recv.at[1, i], lax.rem(me + leaf_count - 1, leaf_count), mine,
            )
        )
        pl.when(me < leaf_count - 1)(to_right[i].start)
        pl.when(me > 0)(to_left[i].start)

    to_right, to_left = [], []
    for i in range(leaf_dev // GW):
        if i == ENTER:
            enter()
            for before in range(i):
                send_leaves(before)
        gather_leaves(i)
        if i >= ENTER:
            send_leaves(i)
    if ENTER == leaf_dev // GW:
        enter()
        for before in range(ENTER):
            send_leaves(before)

    def lift_pair(j):
        first, second = split2(skel[2 * j]), split2(skel[2 * j + 1])
        skel[leaf_dev + j] = dot2(first, local[2 * j, 0]) + dot2(second, local[2 * j + 1, 0])
        field[2 * j + 1] = dot2(first, local[2 * j, 1])
        field[2 * j] = dot2(second, local[2 * j + 1, 1])

    def over_pairs(first, count, step):
        width = min(count, 8)

        def trip(i, carry):
            for u in range(width):
                step(first + i * width + u)
            return carry

        if count == width:
            trip(0, 0)
        else:
            lax.fori_loop(0, count // width, trip, 0)

    def leaf_skeleton(l):
        skel[l] = dot(window[leaf_dev + l, 16:, :], basis[l])

    loads[0].wait()
    several(0, leaf_dev, KW, leaf_skeleton)

    first = 0
    for level in range(levels):
        loads[1 + level].wait()
        count = leaf_dev >> (level + 1)
        over_pairs(first, count, lift_pair)
        first += count

    def spread_chain():
        now2 = split2(skel[2 * leaf_dev - 2])
        copies = []
        for step in range(chain_depth):
            chain_out[step] = dot2(now2, chain[step, 1]).astype(BF16)
            count = 2**step
            place = lax.rem(me, count)
            across = me // count
            across = (across + 1 - 2 * lax.rem(across, 2)) * count
            for k in range(count):
                copies.append(
                    remote(
                        chain_out.at[step], chain_in.at[count - 1 + place],
                        chain_send.at[count - 1 + k], chain_recv.at[count - 1 + place],
                        across + lax.rem(place + k, count), mine,
                    )
                )
                copies[-1].start()
            if step < last:
                now2 = split2(dot2(now2, chain[step, 0]))
        return copies

    loads[1 + levels].wait()

    @pl.when(me > 0)
    def _():
        for copy in to_right:
            copy.wait_recv()

    @pl.when(me < leaf_count - 1)
    def _():
        for copy in to_left:
            copy.wait_recv()

    base_leaf = me * leaf_dev - leaf_dev

    def near_group(i, carry):
        group = [i * NW + u for u in range(NW)]
        own_sides = [target[l] for l in group]
        totals = [jnp.zeros((cols, leaf_size), F32) for _ in group]
        waiting = None
        for n in range(near_count + 1):
            made = []
            if n < near_count:
                for l, own_side in zip(group, own_sides):
                    slot = jnp.clip(blocks[n, l] - base_leaf, 0, 3 * leaf_dev - 1)
                    factor = dot(own_side, window[slot, :16, :])
                    made.append((slot, (1.0 / (factor * factor * factor)).astype(BF16)))
            if waiting:
                for u, (slot, tile) in enumerate(waiting):
                    totals[u] += dot(window[slot, 16:, :], tile, NT)
            waiting = made
        for l, total in zip(group, totals):
            near[l] = total
        return carry

    trips = leaf_dev // NW
    lax.fori_loop(0, FIRST, near_group, 0)
    each_sent(shared, lambda copy: copy.wait_recv())
    each_sent(passed, lambda copy: copy.start())
    lax.fori_loop(FIRST, SECOND, near_group, 0)
    for copy in gathers:
        copy.wait_recv()
    each_passed_in(lambda copy: copy.wait_recv())
    exchange = spread_chain()
    lax.fori_loop(SECOND, trips, near_group, 0)
    for slot in range(leaf_count - 1):
        remote(
            chain_out.at[0], chain_in.at[slot], chain_send.at[slot], chain_recv.at[slot], twin, mine
        ).wait_recv()

    def coupling(step):
        first_slot = 2**step - 1
        total = chain_in[first_slot].astype(F32)
        for slot in range(first_slot + 1, 2 * first_slot + 1):
            total = total + chain_in[slot].astype(F32)
        return total

    node = coupling(last)
    for step in range(last - 1, -1, -1):
        node = coupling(step) + dot2(split2(node), chain[step, 0], NT)
    field[2 * leaf_dev - 2] = node

    def push_pair(j):
        parent = split2(field[leaf_dev + j])
        for child in (2 * j, 2 * j + 1):
            field[child] = field[child] + dot2(parent, local[child, 0], NT)

    for level in range(levels - 1, -1, -1):
        count = leaf_dev >> (level + 1)
        first -= count
        over_pairs(first, count, push_pair)

    def finish_leaf(l):
        out_ref[l] = (near[l] + dot2(split2(field[l]), basis[l], NT)).astype(BF16)

    several(0, leaf_dev, SW, finish_leaf)

    for copy in gathers + exchange:
        copy.wait_send()
    each_sent(shared, lambda copy: copy.wait_send())
    each_sent(passed, lambda copy: copy.wait_send())

    @pl.when(me < leaf_count - 1)
    def _():
        for copy in to_right:
            copy.wait_send()

    @pl.when(me > 0)
    def _():
        for copy in to_left:
            copy.wait_send()


def place_kernel(order_hbm, tree_hbm, out_ref, placed, order, tree, sems):
    loads = [
        pltpu.make_async_copy(order_hbm, order, sems.at[0]),
        pltpu.make_async_copy(tree_hbm, tree, sems.at[1]),
    ]
    for load in loads:
        load.start()
    loads[0].wait()
    leaf_dev, cols, leaf_size = tree.shape
    wide = PW * leaf_size
    row_id = lax.broadcasted_iota(jnp.int32, (leaf_size, wide), 0)
    for i in range(leaf_dev // PW):
        where_to = order[:, i * wide : (i + 1) * wide]
        hot = jnp.where(row_id == where_to % leaf_size, 1.0, 0.0).astype(BF16)
        high = where_to // leaf_size
        if i == 0:
            loads[1].wait()
        mine = jnp.concatenate([tree[i * PW + u].astype(F32) for u in range(PW)], axis=1)
        spread = jnp.concatenate(
            [jnp.where(high == h, mine, 0.0).astype(BF16) for h in range(leaf_dev)], axis=0
        )
        term = dot(spread, hot, NT)
        if i == 0:
            placed[...] = term
        elif i < leaf_dev // PW - 1:
            placed[...] += term
        else:
            for h in range(leaf_dev):
                rows = slice(h * cols, (h + 1) * cols)
                out_ref[:, h * leaf_size : (h + 1) * leaf_size] = placed[rows] + term[rows]


def shards(points, values, order, block_list, leaf_basis, local_transfers, chain_transfers):
    leaf_dev, leaf_size, rank = leaf_basis.shape
    leaf_count = lax.axis_size("leaf")
    probe_count = lax.axis_size("probe")
    depth = leaf_count.bit_length() - 1
    columns = values.shape[0]
    cols = -(-columns // 16) * 16
    if cols != columns:
        values = jnp.pad(values, ((0, cols - columns), (0, 0)))
    dim = points.shape[0]
    levels = leaf_dev.bit_length() - 1
    nodes = 2 * leaf_dev
    vmem = pl.BlockSpec(memory_space=pltpu.VMEM)
    anywhere = pl.BlockSpec(memory_space=pl.ANY)
    tree = pl.pallas_call(
        functools.partial(tree_kernel, leaf_count, probe_count, depth, block_list.shape[1]),
        out_shape=jax.ShapeDtypeStruct((leaf_dev, cols, leaf_size), BF16),
        in_specs=[anywhere] * 7,
        out_specs=vmem,
        scratch_shapes=[
            pltpu.SMEM(block_list.shape[::-1], jnp.int32),
            pltpu.VMEM(points.shape, BF16),
            pltpu.VMEM(values.shape, BF16),
            pltpu.VMEM(order.shape, jnp.int32),
            pltpu.VMEM((leaf_dev * (cols + dim), leaf_size), BF16),
            pltpu.VMEM((leaf_dev, dim, leaf_size), F32),
            pltpu.VMEM((3 * leaf_dev, 16 + cols, leaf_size), BF16),
            pltpu.VMEM((leaf_dev, leaf_size, 16), BF16),
            pltpu.VMEM(leaf_basis.shape, BF16),
            pltpu.VMEM(local_transfers.shape[1:], BF16),
            pltpu.VMEM((depth, 2, rank, rank), BF16),
            pltpu.VMEM((nodes, cols, rank), F32),
            pltpu.VMEM((nodes, cols, rank), F32),
            pltpu.VMEM((leaf_dev, cols, leaf_size), F32),
            pltpu.VMEM((depth, cols, rank), BF16),
            pltpu.VMEM((leaf_count - 1, cols, rank), BF16),
            pltpu.SemaphoreType.DMA((4,)),
            pltpu.SemaphoreType.DMA((levels + 2,)),
            pltpu.SemaphoreType.DMA((probe_count - 1,)),
            pltpu.SemaphoreType.DMA((probe_count - 1,)),
            pltpu.SemaphoreType.DMA(((probe_count - 1) * (depth - 1),)),
            pltpu.SemaphoreType.DMA(((probe_count - 1) * (depth - 1),)),
            pltpu.SemaphoreType.DMA(((probe_count - 1) * (depth - 1),)),
            pltpu.SemaphoreType.DMA(((probe_count - 1) * (depth - 1),)),
            pltpu.SemaphoreType.DMA((2, leaf_dev // GW)),
            pltpu.SemaphoreType.DMA((2, leaf_dev // GW)),
            pltpu.SemaphoreType.DMA((leaf_count - 1,)),
            pltpu.SemaphoreType.DMA((leaf_count - 1,)),
        ],
        compiler_params=pltpu.CompilerParams(
            collective_id=0, has_side_effects=True, vmem_limit_bytes=60 * 1024 * 1024
        ),
        name="tree_product",
    )(block_list.T, points, values, order, leaf_basis, local_transfers[0], chain_transfers[0])
    product = pl.pallas_call(
        place_kernel,
        out_shape=jax.ShapeDtypeStruct((cols, leaf_dev * leaf_size), F32),
        in_specs=[anywhere] * 2,
        out_specs=vmem,
        scratch_shapes=[
            pltpu.VMEM((leaf_dev * cols, leaf_size), F32),
            pltpu.VMEM(order.shape, jnp.int32),
            pltpu.VMEM(tree.shape, BF16),
            pltpu.SemaphoreType.DMA((2,)),
        ],
        compiler_params=pltpu.CompilerParams(vmem_limit_bytes=60 * 1024 * 1024),
        name="place",
    )(order, tree)
    return product[:columns]


def solution(mesh):
    placed = (
        P(None, "leaf"),
        P("probe", "leaf"),
        P("leaf", None),
        P("leaf", None),
        P("leaf", None, None),
        P("leaf", None, None, None, None),
        P("leaf", None, None, "probe", None),
    )
    return jax.shard_map(
        shards, mesh=mesh, in_specs=placed, out_specs=P("probe", "leaf"), check_vma=False
    )
```

```python
import functools

import jax
import jax.numpy as jnp
from jax import lax
from jax.experimental import pallas as pl
from jax.experimental.pallas import tpu as pltpu
from jax.sharding import PartitionSpec as P

F32 = jnp.float32
BF16 = jnp.bfloat16
NN = (((1,), (0,)), ((), ()))
NT = (((1,), (1,)), ((), ()))
GW = 4
NW = 4
SW = 16
KW = 16
PW = 4
ENTER = 0
FIRST = 0
SECOND = 1


def split2(x):
    hi = x.astype(BF16)
    lo = (x - hi.astype(F32)).astype(BF16)
    return jnp.concatenate([hi, lo], axis=0)


def dot(a, b, dims=NN):
    return lax.dot_general(a, b, dims, preferred_element_type=F32)


def dot2(x2, b, dims=NN):
    rows = x2.shape[0] // 2
    out = dot(x2, b, dims)
    return out[:rows] + out[rows:]


def several(first, last, width, step):
    count = (last - first) // width

    def trip(i, carry):
        for u in range(width):
            step(first + i * width + u)
        return carry

    lax.fori_loop(0, count, trip, 0)
    for left in range(first + count * width, last):
        step(left)


def tree_kernel(
    leaf_count, probe_count, chain_depth, near_count,
    blocks_hbm, points_hbm, values_hbm, order_hbm, basis_hbm, local_hbm, chain_hbm,
    out_ref,
    blocks, points, values, order, stacked, coords, window, target, basis, local, chain,
    skel, field, near, chain_out, chain_in,
    first_sem, local_sem, probe_send, probe_recv, share_send, share_recv, pass_send, pass_recv,
    halo_send, halo_recv, chain_send, chain_recv,
):
    leaf_dev, leaf_size, rank = basis.shape
    dim = points.shape[0]
    cols = values.shape[0]
    rows = chain_hbm.shape[2]
    levels = leaf_dev.bit_length() - 1
    me = lax.axis_index("leaf")
    mine = lax.axis_index("probe")

    barrier = pltpu.get_barrier_semaphore()
    for k in range(1, leaf_count):
        pl.semaphore_signal(
            barrier, inc=1,
            device_id=(lax.rem(me + k, leaf_count), mine), device_id_type=pl.DeviceIdType.MESH,
        )
    for k in range(1, probe_count):
        pl.semaphore_signal(
            barrier, inc=1,
            device_id=(me, lax.rem(mine + k, probe_count)), device_id_type=pl.DeviceIdType.MESH,
        )

    arrays = ((values_hbm, values), (points_hbm, points), (order_hbm, order), (blocks_hbm, blocks))
    inputs = [
        pltpu.make_async_copy(src, dst, first_sem.at[i]) for i, (src, dst) in enumerate(arrays)
    ]
    for load in inputs:
        load.start()
    loads = [pltpu.make_async_copy(basis_hbm, basis, local_sem.at[0])]
    start = 0
    for level in range(levels):
        count = leaf_dev >> level
        part = pl.ds(start, count)
        loads.append(
            pltpu.make_async_copy(local_hbm.at[part], local.at[part], local_sem.at[1 + level])
        )
        start += count
    chain_part = chain.at[:, :, pl.ds(pl.multiple_of(mine * rows, rows), rows), :]
    loads.append(pltpu.make_async_copy(chain_hbm, chain_part, local_sem.at[1 + levels]))
    for load in loads[:2]:
        load.start()

    core = lax.rem(me, 2)
    twin = me + 1 - 2 * core
    kind = 1 - core
    last = chain_depth - 1

    def remote(src, dst, send, recv, leaf, probe):
        return pltpu.make_async_remote_copy(
            src_ref=src, dst_ref=dst, send_sem=send, recv_sem=recv,
            device_id=(leaf, probe), device_id_type=pl.DeviceIdType.MESH,
        )

    def rows_of(owner):
        return pl.ds(pl.multiple_of(owner * rows, rows), rows)

    gathers, shared, passed = [], [], []
    for k in range(1, probe_count):
        peer = lax.rem(mine + k, probe_count)
        source = lax.rem(mine + probe_count - k, probe_count)
        for step in range(1, chain_depth):
            slot = (k - 1) * last + step - 1
            shared.append(
                remote(
                    chain_hbm.at[step, kind], chain.at[step, kind, rows_of(mine)],
                    share_send.at[slot], share_recv.at[slot], me, peer,
                )
            )
            arrived = chain.at[step, kind, rows_of(source)]
            passed.append(
                remote(arrived, arrived, pass_send.at[slot], pass_recv.at[slot], twin, mine)
            )
        gathers.append(
            remote(
                chain_hbm.at[0], chain.at[0, :, rows_of(mine)],
                probe_send.at[k - 1], probe_recv.at[k - 1], me, peer,
            )
        )

    def top(i):
        return i % last == last - 1

    def each_sent(copies, act):
        for i, copy in enumerate(copies):
            if not top(i):
                act(copy)

        @pl.when(core == 0)
        def _():
            for i, copy in enumerate(copies):
                if top(i):
                    act(copy)

    def each_passed_in(act):
        for i, copy in enumerate(passed):
            if not top(i):
                act(copy)

        @pl.when(core == 1)
        def _():
            for i, copy in enumerate(passed):
                if top(i):
                    act(copy)


    for load in inputs:
        load.wait()
    for h in range(leaf_dev):
        piece = slice(h * leaf_size, (h + 1) * leaf_size)
        stacked[h * cols : (h + 1) * cols, :] = values[:, piece]
    stacked[leaf_dev * cols :, :] = jnp.concatenate(
        [
            points[:, h * leaf_size : (h + 1) * leaf_size].astype(F32)
            for h in range(leaf_dev)
        ],
        axis=0,
    ).astype(BF16)

    wide = GW * leaf_size
    row_id = lax.broadcasted_iota(jnp.int32, (leaf_size, wide), 0)
    tail_row = lax.broadcasted_iota(jnp.int32, (8, leaf_size), 0)

    def augment(l):
        x = coords[l]
        norm = jnp.sum(x * x, axis=0, keepdims=True) * 0.125
        n1 = norm.astype(BF16).astype(F32)
        n2 = (norm - n1).astype(BF16).astype(F32)
        n3 = norm - n1 - n2
        one = jnp.where(tail_row < 7, 1.0, 0.0)
        src_tail = jnp.where(
            tail_row == 0, n1, jnp.where(tail_row == 1, n2, jnp.where(tail_row == 2, n3, one))
        )
        own_tail = jnp.where(
            tail_row == 3, n1, jnp.where(tail_row == 4, n2, jnp.where(tail_row == 5, n3, one))
        )
        window[leaf_dev + l, :16, :] = jnp.concatenate([x, src_tail], axis=0).astype(BF16)
        target[l] = jnp.concatenate([x * -0.25, own_tail], axis=0).T.astype(BF16)

    def gather_leaves(i):
        piece = slice(i * wide, (i + 1) * wide)
        where_to = order[:, piece]
        low = where_to % leaf_size
        high = where_to // leaf_size
        hot = jnp.where(row_id == low, 1.0, 0.0).astype(BF16)
        found = dot(stacked[...], hot)
        vals = jnp.zeros((cols, wide), F32)
        x = jnp.zeros((dim, wide), F32)
        for h in range(leaf_dev):
            here = high == h
            vals = jnp.where(here, found[h * cols : (h + 1) * cols], vals)
            base = leaf_dev * cols + h * dim
            x = jnp.where(here, found[base : base + dim], x)
        for u in range(GW):
            part = slice(u * leaf_size, (u + 1) * leaf_size)
            coords[i * GW + u] = x[:, part]
            window[leaf_dev + i * GW + u, 16:, :] = vals[:, part].astype(BF16)
            augment(i * GW + u)

    def enter():
        pl.semaphore_wait(barrier, leaf_count - 1 + probe_count - 1)
        each_sent(shared, lambda copy: copy.start())
        for copy in gathers:
            copy.start()
        for load in loads[2:]:
            load.start()

    def send_leaves(i):
        own = window.at[pl.ds(leaf_dev + i * GW, GW)]
        to_right.append(
            remote(
                own, window.at[pl.ds(i * GW, GW)], halo_send.at[0, i], halo_recv.at[0, i],
                lax.rem(me + 1, leaf_count), mine,
            )
        )
        to_left.append(
            remote(
                own, window.at[pl.ds(2 * leaf_dev + i * GW, GW)], halo_send.at[1, i],
                halo_recv.at[1, i], lax.rem(me + leaf_count - 1, leaf_count), mine,
            )
        )
        pl.when(me < leaf_count - 1)(to_right[i].start)
        pl.when(me > 0)(to_left[i].start)

    to_right, to_left = [], []
    for i in range(leaf_dev // GW):
        if i == ENTER:
            enter()
            for before in range(i):
                send_leaves(before)
        gather_leaves(i)
        if i >= ENTER:
            send_leaves(i)
    if ENTER == leaf_dev // GW:
        enter()
        for before in range(ENTER):
            send_leaves(before)

    def lift_pair(j):
        first, second = split2(skel[2 * j]), split2(skel[2 * j + 1])
        skel[leaf_dev + j] = dot2(first, local[2 * j, 0]) + dot2(second, local[2 * j + 1, 0])
        field[2 * j + 1] = dot2(first, local[2 * j, 1])
        field[2 * j] = dot2(second, local[2 * j + 1, 1])

    def over_pairs(first, count, step):
        width = min(count, 8)

        def trip(i, carry):
            for u in range(width):
                step(first + i * width + u)
            return carry

        if count == width:
            trip(0, 0)
        else:
            lax.fori_loop(0, count // width, trip, 0)

    def leaf_skeleton(l):
        skel[l] = dot(window[leaf_dev + l, 16:, :], basis[l])

    loads[0].wait()
    several(0, leaf_dev, KW, leaf_skeleton)

    first = 0
    for level in range(levels):
        loads[1 + level].wait()
        count = leaf_dev >> (level + 1)
        over_pairs(first, count, lift_pair)
        first += count

    def spread_chain():
        lifted = [split2(skel[2 * leaf_dev - 2])]
        for step in range(last):
            lifted.append(split2(dot2(lifted[step], chain[step, 0])))
        copies = []
        for step in range(last, -1, -1):
            chain_out[step] = dot2(lifted[step], chain[step, 1]).astype(BF16)
            count = 2**step
            place = lax.rem(me, count)
            across = me // count
            across = (across + 1 - 2 * lax.rem(across, 2)) * count
            for k in range(count):
                copies.append(
                    remote(
                        chain_out.at[step], chain_in.at[count - 1 + place],
                        chain_send.at[count - 1 + k], chain_recv.at[count - 1 + place],
                        across + lax.rem(place + k, count), mine,
                    )
                )
                copies[-1].start()
        return copies

    loads[1 + levels].wait()

    @pl.when(me > 0)
    def _():
        for copy in to_right:
            copy.wait_recv()

    @pl.when(me < leaf_count - 1)
    def _():
        for copy in to_left:
            copy.wait_recv()

    base_leaf = me * leaf_dev - leaf_dev

    def near_group(i, carry):
        group = [i * NW + u for u in range(NW)]
        own_sides = [target[l] for l in group]
        totals = [jnp.zeros((cols, leaf_size), F32) for _ in group]
        waiting = None
        for n in range(near_count + 1):
            made = []
            if n < near_count:
                for l, own_side in zip(group, own_sides):
                    slot = jnp.clip(blocks[n, l] - base_leaf, 0, 3 * leaf_dev - 1)
                    factor = dot(own_side, window[slot, :16, :])
                    made.append((slot, (1.0 / (factor * factor * factor)).astype(BF16)))
            if waiting:
                for u, (slot, tile) in enumerate(waiting):
                    totals[u] += dot(window[slot, 16:, :], tile, NT)
            waiting = made
        for l, total in zip(group, totals):
            near[l] = total
        return carry

    trips = leaf_dev // NW
    lax.fori_loop(0, FIRST, near_group, 0)
    each_sent(shared, lambda copy: copy.wait_recv())
    each_sent(passed, lambda copy: copy.start())
    lax.fori_loop(FIRST, SECOND, near_group, 0)
    for copy in gathers:
        copy.wait_recv()
    each_passed_in(lambda copy: copy.wait_recv())
    exchange = spread_chain()
    lax.fori_loop(SECOND, trips, near_group, 0)
    for slot in range(leaf_count - 1):
        remote(
            chain_out.at[0], chain_in.at[slot], chain_send.at[slot], chain_recv.at[slot], twin, mine
        ).wait_recv()

    def coupling(step):
        first_slot = 2**step - 1
        total = chain_in[first_slot].astype(F32)
        for slot in range(first_slot + 1, 2 * first_slot + 1):
            total = total + chain_in[slot].astype(F32)
        return total

    node = coupling(last)
    for step in range(last - 1, -1, -1):
        node = coupling(step) + dot2(split2(node), chain[step, 0], NT)
    field[2 * leaf_dev - 2] = node

    def push_pair(j):
        parent = split2(field[leaf_dev + j])
        for child in (2 * j, 2 * j + 1):
            field[child] = field[child] + dot2(parent, local[child, 0], NT)

    for level in range(levels - 1, -1, -1):
        count = leaf_dev >> (level + 1)
        first -= count
        over_pairs(first, count, push_pair)

    def finish_leaf(l):
        out_ref[l] = (near[l] + dot2(split2(field[l]), basis[l], NT)).astype(BF16)

    several(0, leaf_dev, SW, finish_leaf)

    for copy in gathers + exchange:
        copy.wait_send()
    each_sent(shared, lambda copy: copy.wait_send())
    each_sent(passed, lambda copy: copy.wait_send())

    @pl.when(me < leaf_count - 1)
    def _():
        for copy in to_right:
            copy.wait_send()

    @pl.when(me > 0)
    def _():
        for copy in to_left:
            copy.wait_send()


def place_kernel(order_hbm, tree_hbm, out_ref, placed, order, tree, sems):
    loads = [
        pltpu.make_async_copy(order_hbm, order, sems.at[0]),
        pltpu.make_async_copy(tree_hbm, tree, sems.at[1]),
    ]
    for load in loads:
        load.start()
    loads[0].wait()
    leaf_dev, cols, leaf_size = tree.shape
    wide = PW * leaf_size
    row_id = lax.broadcasted_iota(jnp.int32, (leaf_size, wide), 0)
    for i in range(leaf_dev // PW):
        where_to = order[:, i * wide : (i + 1) * wide]
        hot = jnp.where(row_id == where_to % leaf_size, 1.0, 0.0).astype(BF16)
        high = where_to // leaf_size
        if i == 0:
            loads[1].wait()
        mine = jnp.concatenate([tree[i * PW + u].astype(F32) for u in range(PW)], axis=1)
        spread = jnp.concatenate(
            [jnp.where(high == h, mine, 0.0).astype(BF16) for h in range(leaf_dev)], axis=0
        )
        term = dot(spread, hot, NT)
        if i == 0:
            placed[...] = term
        elif i < leaf_dev // PW - 1:
            placed[...] += term
        else:
            for h in range(leaf_dev):
                rows = slice(h * cols, (h + 1) * cols)
                out_ref[:, h * leaf_size : (h + 1) * leaf_size] = placed[rows] + term[rows]


def shards(points, values, order, block_list, leaf_basis, local_transfers, chain_transfers):
    leaf_dev, leaf_size, rank = leaf_basis.shape
    leaf_count = lax.axis_size("leaf")
    probe_count = lax.axis_size("probe")
    depth = leaf_count.bit_length() - 1
    columns = values.shape[0]
    cols = -(-columns // 16) * 16
    if cols != columns:
        values = jnp.pad(values, ((0, cols - columns), (0, 0)))
    dim = points.shape[0]
    levels = leaf_dev.bit_length() - 1
    nodes = 2 * leaf_dev
    vmem = pl.BlockSpec(memory_space=pltpu.VMEM)
    anywhere = pl.BlockSpec(memory_space=pl.ANY)
    tree = pl.pallas_call(
        functools.partial(tree_kernel, leaf_count, probe_count, depth, block_list.shape[1]),
        out_shape=jax.ShapeDtypeStruct((leaf_dev, cols, leaf_size), BF16),
        in_specs=[anywhere] * 7,
        out_specs=vmem,
        scratch_shapes=[
            pltpu.SMEM(block_list.shape[::-1], jnp.int32),
            pltpu.VMEM(points.shape, BF16),
            pltpu.VMEM(values.shape, BF16),
            pltpu.VMEM(order.shape, jnp.int32),
            pltpu.VMEM((leaf_dev * (cols + dim), leaf_size), BF16),
            pltpu.VMEM((leaf_dev, dim, leaf_size), F32),
            pltpu.VMEM((3 * leaf_dev, 16 + cols, leaf_size), BF16),
            pltpu.VMEM((leaf_dev, leaf_size, 16), BF16),
            pltpu.VMEM(leaf_basis.shape, BF16),
            pltpu.VMEM(local_transfers.shape[1:], BF16),
            pltpu.VMEM((depth, 2, rank, rank), BF16),
            pltpu.VMEM((nodes, cols, rank), F32),
            pltpu.VMEM((nodes, cols, rank), F32),
            pltpu.VMEM((leaf_dev, cols, leaf_size), F32),
            pltpu.VMEM((depth, cols, rank), BF16),
            pltpu.VMEM((leaf_count - 1, cols, rank), BF16),
            pltpu.SemaphoreType.DMA((4,)),
            pltpu.SemaphoreType.DMA((levels + 2,)),
            pltpu.SemaphoreType.DMA((probe_count - 1,)),
            pltpu.SemaphoreType.DMA((probe_count - 1,)),
            pltpu.SemaphoreType.DMA(((probe_count - 1) * (depth - 1),)),
            pltpu.SemaphoreType.DMA(((probe_count - 1) * (depth - 1),)),
            pltpu.SemaphoreType.DMA(((probe_count - 1) * (depth - 1),)),
            pltpu.SemaphoreType.DMA(((probe_count - 1) * (depth - 1),)),
            pltpu.SemaphoreType.DMA((2, leaf_dev // GW)),
            pltpu.SemaphoreType.DMA((2, leaf_dev // GW)),
            pltpu.SemaphoreType.DMA((leaf_count - 1,)),
            pltpu.SemaphoreType.DMA((leaf_count - 1,)),
        ],
        compiler_params=pltpu.CompilerParams(
            collective_id=0, has_side_effects=True, vmem_limit_bytes=60 * 1024 * 1024
        ),
        name="tree_product",
    )(block_list.T, points, values, order, leaf_basis, local_transfers[0], chain_transfers[0])
    product = pl.pallas_call(
        place_kernel,
        out_shape=jax.ShapeDtypeStruct((cols, leaf_dev * leaf_size), F32),
        in_specs=[anywhere] * 2,
        out_specs=vmem,
        scratch_shapes=[
            pltpu.VMEM((leaf_dev * cols, leaf_size), F32),
            pltpu.VMEM(order.shape, jnp.int32),
            pltpu.VMEM(tree.shape, BF16),
            pltpu.SemaphoreType.DMA((2,)),
        ],
        compiler_params=pltpu.CompilerParams(vmem_limit_bytes=60 * 1024 * 1024),
        name="place",
    )(order, tree)
    return product[:columns]


def solution(mesh):
    placed = (
        P(None, "leaf"),
        P("probe", "leaf"),
        P("leaf", None),
        P("leaf", None),
        P("leaf", None, None),
        P("leaf", None, None, None, None),
        P("leaf", None, None, "probe", None),
    )
    return jax.shard_map(
        shards, mesh=mesh, in_specs=placed, out_specs=P("probe", "leaf"), check_vma=False
    )
```

```python
import functools

import jax
import jax.numpy as jnp
from jax import lax
from jax.experimental import pallas as pl
from jax.experimental.pallas import tpu as pltpu
from jax.sharding import PartitionSpec as P

F32 = jnp.float32
BF16 = jnp.bfloat16
NN = (((1,), (0,)), ((), ()))
NT = (((1,), (1,)), ((), ()))
GW = 4
SW = 16
KW = 16
PW = 4
ENTER = 0


def split2(x):
    hi = x.astype(BF16)
    lo = (x - hi.astype(F32)).astype(BF16)
    return jnp.concatenate([hi, lo], axis=0)


def dot(a, b, dims=NN):
    return lax.dot_general(a, b, dims, preferred_element_type=F32)


def dot2(x2, b, dims=NN):
    rows = x2.shape[0] // 2
    out = dot(x2, b, dims)
    return out[:rows] + out[rows:]


def several(first, last, width, step):
    count = (last - first) // width

    def trip(i, carry):
        for u in range(width):
            step(first + i * width + u)
        return carry

    lax.fori_loop(0, count, trip, 0)
    for left in range(first + count * width, last):
        step(left)


def tree_kernel(
    leaf_count, probe_count, chain_depth, near_count,
    blocks_hbm, points_hbm, values_hbm, order_hbm, basis_hbm, local_hbm, chain_hbm,
    out_ref,
    blocks, points, values, order, stacked, coords, window, target, basis, local, chain,
    skel, field, near, chain_out, chain_in,
    first_sem, local_sem, probe_send, probe_recv, share_send, share_recv, pass_send, pass_recv,
    halo_send, halo_recv, chain_send, chain_recv,
):
    leaf_dev, leaf_size, rank = basis.shape
    dim = points.shape[0]
    cols = values.shape[0]
    rows = chain_hbm.shape[2]
    levels = leaf_dev.bit_length() - 1
    me = lax.axis_index("leaf")
    mine = lax.axis_index("probe")

    barrier = pltpu.get_barrier_semaphore()
    for k in range(1, leaf_count):
        pl.semaphore_signal(
            barrier, inc=1,
            device_id=(lax.rem(me + k, leaf_count), mine), device_id_type=pl.DeviceIdType.MESH,
        )
    for k in range(1, probe_count):
        pl.semaphore_signal(
            barrier, inc=1,
            device_id=(me, lax.rem(mine + k, probe_count)), device_id_type=pl.DeviceIdType.MESH,
        )

    arrays = ((values_hbm, values), (points_hbm, points), (order_hbm, order), (blocks_hbm, blocks))
    inputs = [
        pltpu.make_async_copy(src, dst, first_sem.at[i]) for i, (src, dst) in enumerate(arrays)
    ]
    for load in inputs:
        load.start()
    loads = [pltpu.make_async_copy(basis_hbm, basis, local_sem.at[0])]
    start = 0
    for level in range(levels):
        count = leaf_dev >> level
        part = pl.ds(start, count)
        loads.append(
            pltpu.make_async_copy(local_hbm.at[part], local.at[part], local_sem.at[1 + level])
        )
        start += count
    chain_part = chain.at[:, :, pl.ds(pl.multiple_of(mine * rows, rows), rows), :]
    loads.append(pltpu.make_async_copy(chain_hbm, chain_part, local_sem.at[1 + levels]))
    for load in loads[:2]:
        load.start()

    core = lax.rem(me, 2)
    twin = me + 1 - 2 * core
    kind = 1 - core
    last = chain_depth - 1

    def remote(src, dst, send, recv, leaf, probe):
        return pltpu.make_async_remote_copy(
            src_ref=src, dst_ref=dst, send_sem=send, recv_sem=recv,
            device_id=(leaf, probe), device_id_type=pl.DeviceIdType.MESH,
        )

    def rows_of(owner):
        return pl.ds(pl.multiple_of(owner * rows, rows), rows)

    gathers, shared, passed = [], [], []
    for k in range(1, probe_count):
        peer = lax.rem(mine + k, probe_count)
        source = lax.rem(mine + probe_count - k, probe_count)
        for step in range(1, chain_depth):
            slot = (k - 1) * last + step - 1
            shared.append(
                remote(
                    chain_hbm.at[step, kind], chain.at[step, kind, rows_of(mine)],
                    share_send.at[slot], share_recv.at[slot], me, peer,
                )
            )
            arrived = chain.at[step, kind, rows_of(source)]
            passed.append(
                remote(arrived, arrived, pass_send.at[slot], pass_recv.at[slot], twin, mine)
            )
        gathers.append(
            remote(
                chain_hbm.at[0], chain.at[0, :, rows_of(mine)],
                probe_send.at[k - 1], probe_recv.at[k - 1], me, peer,
            )
        )

    def top(i):
        return i % last == last - 1

    def each_sent(copies, act):
        for i, copy in enumerate(copies):
            if not top(i):
                act(copy)

        @pl.when(core == 0)
        def _():
            for i, copy in enumerate(copies):
                if top(i):
                    act(copy)

    def each_passed_in(act):
        for i, copy in enumerate(passed):
            if not top(i):
                act(copy)

        @pl.when(core == 1)
        def _():
            for i, copy in enumerate(passed):
                if top(i):
                    act(copy)


    for load in inputs:
        load.wait()
    for h in range(leaf_dev):
        piece = slice(h * leaf_size, (h + 1) * leaf_size)
        stacked[h * cols : (h + 1) * cols, :] = values[:, piece]
    stacked[leaf_dev * cols :, :] = jnp.concatenate(
        [
            points[:, h * leaf_size : (h + 1) * leaf_size].astype(F32)
            for h in range(leaf_dev)
        ],
        axis=0,
    ).astype(BF16)

    wide = GW * leaf_size
    row_id = lax.broadcasted_iota(jnp.int32, (leaf_size, wide), 0)
    tail_row = lax.broadcasted_iota(jnp.int32, (8, leaf_size), 0)

    def augment(l):
        x = coords[l]
        norm = jnp.sum(x * x, axis=0, keepdims=True) * 0.125
        n1 = norm.astype(BF16).astype(F32)
        n2 = (norm - n1).astype(BF16).astype(F32)
        n3 = norm - n1 - n2
        one = jnp.where(tail_row < 7, 1.0, 0.0)
        src_tail = jnp.where(
            tail_row == 0, n1, jnp.where(tail_row == 1, n2, jnp.where(tail_row == 2, n3, one))
        )
        own_tail = jnp.where(
            tail_row == 3, n1, jnp.where(tail_row == 4, n2, jnp.where(tail_row == 5, n3, one))
        )
        window[leaf_dev + l, :16, :] = jnp.concatenate([x, src_tail], axis=0).astype(BF16)
        target[l] = jnp.concatenate([x * -0.25, own_tail], axis=0).T.astype(BF16)

    def gather_leaves(i):
        piece = slice(i * wide, (i + 1) * wide)
        where_to = order[:, piece]
        low = where_to % leaf_size
        high = where_to // leaf_size
        hot = jnp.where(row_id == low, 1.0, 0.0).astype(BF16)
        found = dot(stacked[...], hot)
        vals = jnp.zeros((cols, wide), F32)
        x = jnp.zeros((dim, wide), F32)
        for h in range(leaf_dev):
            here = high == h
            vals = jnp.where(here, found[h * cols : (h + 1) * cols], vals)
            base = leaf_dev * cols + h * dim
            x = jnp.where(here, found[base : base + dim], x)
        for u in range(GW):
            part = slice(u * leaf_size, (u + 1) * leaf_size)
            coords[i * GW + u] = x[:, part]
            window[leaf_dev + i * GW + u, 16:, :] = vals[:, part].astype(BF16)
            augment(i * GW + u)

    def enter():
        pl.semaphore_wait(barrier, leaf_count - 1 + probe_count - 1)
        each_sent(shared, lambda copy: copy.start())
        for copy in gathers:
            copy.start()
        for load in loads[2:]:
            load.start()

    def send_leaves(i):
        own = window.at[pl.ds(leaf_dev + i * GW, GW)]
        to_right.append(
            remote(
                own, window.at[pl.ds(i * GW, GW)], halo_send.at[0, i], halo_recv.at[0, i],
                lax.rem(me + 1, leaf_count), mine,
            )
        )
        to_left.append(
            remote(
                own, window.at[pl.ds(2 * leaf_dev + i * GW, GW)], halo_send.at[1, i],
                halo_recv.at[1, i], lax.rem(me + leaf_count - 1, leaf_count), mine,
            )
        )
        pl.when(me < leaf_count - 1)(to_right[i].start)
        pl.when(me > 0)(to_left[i].start)

    to_right, to_left = [], []
    for i in range(leaf_dev // GW):
        if i == ENTER:
            enter()
            for before in range(i):
                send_leaves(before)
        gather_leaves(i)
        if i >= ENTER:
            send_leaves(i)
    if ENTER == leaf_dev // GW:
        enter()
        for before in range(ENTER):
            send_leaves(before)

    def lift_pair(j):
        first, second = split2(skel[2 * j]), split2(skel[2 * j + 1])
        skel[leaf_dev + j] = dot2(first, local[2 * j, 0]) + dot2(second, local[2 * j + 1, 0])
        field[2 * j + 1] = dot2(first, local[2 * j, 1])
        field[2 * j] = dot2(second, local[2 * j + 1, 1])

    def over_pairs(first, count, step):
        width = min(count, 8)

        def trip(i, carry):
            for u in range(width):
                step(first + i * width + u)
            return carry

        if count == width:
            trip(0, 0)
        else:
            lax.fori_loop(0, count // width, trip, 0)

    def leaf_skeleton(l):
        skel[l] = dot(window[leaf_dev + l, 16:, :], basis[l])

    loads[0].wait()
    several(0, leaf_dev, KW, leaf_skeleton)

    first = 0
    for level in range(levels):
        loads[1 + level].wait()
        count = leaf_dev >> (level + 1)
        over_pairs(first, count, lift_pair)
        first += count

    def spread_chain():
        lifted = [split2(skel[2 * leaf_dev - 2])]
        for step in range(last):
            lifted.append(split2(dot2(lifted[step], chain[step, 0])))
        copies = []
        for step in range(last, -1, -1):
            chain_out[step] = dot2(lifted[step], chain[step, 1]).astype(BF16)
            count = 2**step
            place = lax.rem(me, count)
            across = me // count
            across = (across + 1 - 2 * lax.rem(across, 2)) * count
            for k in range(count):
                copies.append(
                    remote(
                        chain_out.at[step], chain_in.at[count - 1 + place],
                        chain_send.at[count - 1 + k], chain_recv.at[count - 1 + place],
                        across + lax.rem(place + k, count), mine,
                    )
                )
                copies[-1].start()
        return copies

    loads[1 + levels].wait()

    @pl.when(me > 0)
    def _():
        for copy in to_right:
            copy.wait_recv()

    @pl.when(me < leaf_count - 1)
    def _():
        for copy in to_left:
            copy.wait_recv()

    base_leaf = me * leaf_dev - leaf_dev

    def near_leaves(first, width):
        group = [first + u for u in range(width)]
        own_sides = [target[l] for l in group]
        totals = [jnp.zeros((cols, leaf_size), F32) for _ in group]
        waiting = None
        for n in range(near_count + 1):
            made = []
            if n < near_count:
                for l, own_side in zip(group, own_sides):
                    slot = jnp.clip(blocks[n, l] - base_leaf, 0, 3 * leaf_dev - 1)
                    factor = dot(own_side, window[slot, :16, :])
                    made.append((slot, (1.0 / (factor * factor * factor)).astype(BF16)))
            if waiting:
                for u, (slot, tile) in enumerate(waiting):
                    totals[u] += dot(window[slot, 16:, :], tile, NT)
            waiting = made
        for l, total in zip(group, totals):
            near[l] = total

    each_sent(shared, lambda copy: copy.wait_recv())
    each_sent(passed, lambda copy: copy.start())
    def run(first, width, count):
        def trip(i, carry):
            near_leaves(first + i * width, width)
            return carry

        lax.fori_loop(0, count, trip, 0)

    lead = leaf_dev * 3 // 8
    lead += (leaf_dev - lead) % 2
    run(0, lead, 1)
    for copy in gathers:
        copy.wait_recv()
    each_passed_in(lambda copy: copy.wait_recv())
    exchange = spread_chain()
    run(lead, (leaf_dev - lead) // 2, 2)
    for slot in range(leaf_count - 1):
        remote(
            chain_out.at[0], chain_in.at[slot], chain_send.at[slot], chain_recv.at[slot], twin, mine
        ).wait_recv()

    def coupling(step):
        first_slot = 2**step - 1
        total = chain_in[first_slot].astype(F32)
        for slot in range(first_slot + 1, 2 * first_slot + 1):
            total = total + chain_in[slot].astype(F32)
        return total

    node = coupling(last)
    for step in range(last - 1, -1, -1):
        node = coupling(step) + dot2(split2(node), chain[step, 0], NT)
    field[2 * leaf_dev - 2] = node

    def push_pair(j):
        parent = split2(field[leaf_dev + j])
        for child in (2 * j, 2 * j + 1):
            field[child] = field[child] + dot2(parent, local[child, 0], NT)

    for level in range(levels - 1, -1, -1):
        count = leaf_dev >> (level + 1)
        first -= count
        over_pairs(first, count, push_pair)

    def finish_leaf(l):
        out_ref[l] = (near[l] + dot2(split2(field[l]), basis[l], NT)).astype(BF16)

    several(0, leaf_dev, SW, finish_leaf)

    for copy in gathers + exchange:
        copy.wait_send()
    each_sent(shared, lambda copy: copy.wait_send())
    each_sent(passed, lambda copy: copy.wait_send())

    @pl.when(me < leaf_count - 1)
    def _():
        for copy in to_right:
            copy.wait_send()

    @pl.when(me > 0)
    def _():
        for copy in to_left:
            copy.wait_send()


def place_kernel(order_hbm, tree_hbm, out_ref, placed, order, tree, sems):
    loads = [
        pltpu.make_async_copy(order_hbm, order, sems.at[0]),
        pltpu.make_async_copy(tree_hbm, tree, sems.at[1]),
    ]
    for load in loads:
        load.start()
    loads[0].wait()
    leaf_dev, cols, leaf_size = tree.shape
    wide = PW * leaf_size
    row_id = lax.broadcasted_iota(jnp.int32, (leaf_size, wide), 0)
    for i in range(leaf_dev // PW):
        where_to = order[:, i * wide : (i + 1) * wide]
        hot = jnp.where(row_id == where_to % leaf_size, 1.0, 0.0).astype(BF16)
        high = where_to // leaf_size
        if i == 0:
            loads[1].wait()
        mine = jnp.concatenate([tree[i * PW + u].astype(F32) for u in range(PW)], axis=1)
        spread = jnp.concatenate(
            [jnp.where(high == h, mine, 0.0).astype(BF16) for h in range(leaf_dev)], axis=0
        )
        term = dot(spread, hot, NT)
        if i == 0:
            placed[...] = term
        elif i < leaf_dev // PW - 1:
            placed[...] += term
        else:
            for h in range(leaf_dev):
                rows = slice(h * cols, (h + 1) * cols)
                out_ref[:, h * leaf_size : (h + 1) * leaf_size] = placed[rows] + term[rows]


def shards(points, values, order, block_list, leaf_basis, local_transfers, chain_transfers):
    leaf_dev, leaf_size, rank = leaf_basis.shape
    leaf_count = lax.axis_size("leaf")
    probe_count = lax.axis_size("probe")
    depth = leaf_count.bit_length() - 1
    columns = values.shape[0]
    cols = -(-columns // 16) * 16
    if cols != columns:
        values = jnp.pad(values, ((0, cols - columns), (0, 0)))
    dim = points.shape[0]
    levels = leaf_dev.bit_length() - 1
    nodes = 2 * leaf_dev
    vmem = pl.BlockSpec(memory_space=pltpu.VMEM)
    anywhere = pl.BlockSpec(memory_space=pl.ANY)
    tree = pl.pallas_call(
        functools.partial(tree_kernel, leaf_count, probe_count, depth, block_list.shape[1]),
        out_shape=jax.ShapeDtypeStruct((leaf_dev, cols, leaf_size), BF16),
        in_specs=[anywhere] * 7,
        out_specs=vmem,
        scratch_shapes=[
            pltpu.SMEM(block_list.shape[::-1], jnp.int32),
            pltpu.VMEM(points.shape, BF16),
            pltpu.VMEM(values.shape, BF16),
            pltpu.VMEM(order.shape, jnp.int32),
            pltpu.VMEM((leaf_dev * (cols + dim), leaf_size), BF16),
            pltpu.VMEM((leaf_dev, dim, leaf_size), F32),
            pltpu.VMEM((3 * leaf_dev, 16 + cols, leaf_size), BF16),
            pltpu.VMEM((leaf_dev, leaf_size, 16), BF16),
            pltpu.VMEM(leaf_basis.shape, BF16),
            pltpu.VMEM(local_transfers.shape[1:], BF16),
            pltpu.VMEM((depth, 2, rank, rank), BF16),
            pltpu.VMEM((nodes, cols, rank), F32),
            pltpu.VMEM((nodes, cols, rank), F32),
            pltpu.VMEM((leaf_dev, cols, leaf_size), F32),
            pltpu.VMEM((depth, cols, rank), BF16),
            pltpu.VMEM((leaf_count - 1, cols, rank), BF16),
            pltpu.SemaphoreType.DMA((4,)),
            pltpu.SemaphoreType.DMA((levels + 2,)),
            pltpu.SemaphoreType.DMA((probe_count - 1,)),
            pltpu.SemaphoreType.DMA((probe_count - 1,)),
            pltpu.SemaphoreType.DMA(((probe_count - 1) * (depth - 1),)),
            pltpu.SemaphoreType.DMA(((probe_count - 1) * (depth - 1),)),
            pltpu.SemaphoreType.DMA(((probe_count - 1) * (depth - 1),)),
            pltpu.SemaphoreType.DMA(((probe_count - 1) * (depth - 1),)),
            pltpu.SemaphoreType.DMA((2, leaf_dev // GW)),
            pltpu.SemaphoreType.DMA((2, leaf_dev // GW)),
            pltpu.SemaphoreType.DMA((leaf_count - 1,)),
            pltpu.SemaphoreType.DMA((leaf_count - 1,)),
        ],
        compiler_params=pltpu.CompilerParams(
            collective_id=0, has_side_effects=True, vmem_limit_bytes=60 * 1024 * 1024
        ),
        name="tree_product",
    )(block_list.T, points, values, order, leaf_basis, local_transfers[0], chain_transfers[0])
    product = pl.pallas_call(
        place_kernel,
        out_shape=jax.ShapeDtypeStruct((cols, leaf_dev * leaf_size), F32),
        in_specs=[anywhere] * 2,
        out_specs=vmem,
        scratch_shapes=[
            pltpu.VMEM((leaf_dev * cols, leaf_size), F32),
            pltpu.VMEM(order.shape, jnp.int32),
            pltpu.VMEM(tree.shape, BF16),
            pltpu.SemaphoreType.DMA((2,)),
        ],
        compiler_params=pltpu.CompilerParams(vmem_limit_bytes=60 * 1024 * 1024),
        name="place",
    )(order, tree)
    return product[:columns]


def solution(mesh):
    placed = (
        P(None, "leaf"),
        P("probe", "leaf"),
        P("leaf", None),
        P("leaf", None),
        P("leaf", None, None),
        P("leaf", None, None, None, None),
        P("leaf", None, None, "probe", None),
    )
    return jax.shard_map(
        shards, mesh=mesh, in_specs=placed, out_specs=P("probe", "leaf"), check_vma=False
    )
```
